256 devices in a mesh: region: 64 (over z, y, core), nbr: 4 (over x).
Axes of the slice: x: 4, y: 4, z: 8, core: 2. Of those that a mesh axis runs over, the one named last changes fastest.
Arguments:
- interface_op: bfloat16 [64, 4, 2, 1024, 1024], P('region', 'nbr'), may hold values from -0.1875 to 0.1875
- mortar: bfloat16 [64, 4, 4, 2, 256, 256], P('region', 'nbr'), may hold values from -0.375 to 0.375
- source: float32 [64, 4, 2, 1024, 256], P('region', 'nbr'), may hold values from -6 to 6
- trace_len: int32 [64, 4, 4], P('region', 'nbr'), may hold values from 64 to 256
- corner_rows: int32 [64, 4, 8], P('region', 'nbr'), may hold values from 0 to 1023
- corner_owner: int32 [64, 4, 8], P('region', 'nbr'), may hold values from 0 to 255
- coarse_inv: float32 [2, 256, 256], replicated, may hold values from -0.375 to 0.375
Outputs:
- final_field: float32 [64, 4, 2, 1024, 256], P('region', 'nbr')
- increments: float32 [3, 256], replicated
The draws below stay inside these ranges and needn't reach their ends.
Inputs may be any that keep to these rules, and one draw needn't show every extreme that they name: `trace_len`: rows of a face at or beyond its length carry no trace. `corner_rows`: corners of one subdomain may repeat an unknown.
All inputs are finite; a program needn't handle non-finite values.
Results may differ from the reference program's by a relative error of at most 0.0045.
Values may be sent and summed in bfloat16 or wider, within the bound.
No kernel may reach another device: no remote copies, remote signals or barrier semaphores. Data moves between devices by JAX's collectives and lax.ppermute only.
A program may use at most 128 MiB of HBM per device.

```python
import jax
import jax.numpy as jnp
from jax import lax

ORDER = 1024
FACE = 256
PORTS = 256
CORNERS = 8
ITERS = 3
SUB_ROWS = 64
SUB_COLS = 4
COARSE = 256


def with_ends(entries, key, least, top_value):
    spot = [jax.random.randint(jax.random.fold_in(key, axis), (), 0, length) for axis, length in enumerate(entries.shape)]
    longest = entries.shape.index(max(entries.shape))
    neighbour = spot[:longest] + [(spot[longest] + 1) % entries.shape[longest]] + spot[longest + 1:]
    return entries.at[tuple(spot)].set(least).at[tuple(neighbour)].set(top_value)


def level_of(key, extent, cuts, smallest, high):
    level, own = 1.0, jax.random.fold_in(key, 6)
    for dim, blocks in cuts:
        heights = jnp.exp(jax.random.uniform(jax.random.fold_in(own, dim), (blocks,), jnp.float32, smallest / len(cuts), high / len(cuts)))
        level = level * jnp.repeat(heights, extent[dim] // blocks).reshape([-1 if axis == dim else 1 for axis in range(len(extent))])
    return level


def scatter_about(own_key, extent, deviation, reach, cuts=(), kind=jnp.bfloat16):
    loudness = level_of(own_key, extent, cuts, -0.22, 0.18) if cuts else 1.0
    array = jax.random.normal(own_key, extent, jnp.float32) * deviation * loudness
    return jnp.minimum(jnp.maximum(array, -reach), reach).astype(kind)


def setup_inputs(seed: int = 0) -> dict:
    keys = jax.random.split(jax.random.key(seed), 8)
    return {
        "interface_op": scatter_about(keys[0], (SUB_ROWS, SUB_COLS, 2, ORDER, ORDER), ORDER ** -0.5, 0.1875, ((0, 64), (1, 4))),
        "mortar": scatter_about(keys[1], (SUB_ROWS, SUB_COLS, 4, 2, FACE, FACE), FACE ** -0.5, 0.375, ((0, 64), (1, 4))),
        "source": scatter_about(keys[2], (SUB_ROWS, SUB_COLS, 2, ORDER, PORTS), 1.0, 6.0, ((0, 64), (1, 4)), jnp.float32),
        "trace_len": with_ends(jax.random.randint(keys[3], (SUB_ROWS, SUB_COLS, 4), FACE // 4, FACE + 1), jax.random.fold_in(keys[3], 1), FACE // 4, FACE).astype(jnp.int32),
        "corner_rows": with_ends(jax.random.randint(keys[4], (SUB_ROWS, SUB_COLS, CORNERS), 0, ORDER), jax.random.fold_in(keys[4], 1), 0, ORDER - 1).astype(jnp.int32),
        "corner_owner": with_ends(jax.random.randint(keys[5], (SUB_ROWS, SUB_COLS, CORNERS), 0, COARSE), jax.random.fold_in(keys[5], 1), 0, COARSE - 1).astype(jnp.int32),
        "coarse_inv": scatter_about(keys[6], (2, COARSE, COARSE), COARSE ** -0.5, 0.375, (), jnp.float32),
    }


def complex_dot(left, right, accuracy=None):
    real_part = jnp.dot(left[0], right[0], preferred_element_type=jnp.float32, precision=accuracy) - jnp.dot(left[1], right[1], preferred_element_type=jnp.float32, precision=accuracy)
    imag_part = jnp.dot(left[0], right[1], preferred_element_type=jnp.float32, precision=accuracy) + jnp.dot(left[1], right[0], preferred_element_type=jnp.float32, precision=accuracy)
    return jnp.stack([real_part, imag_part])


def mortar_apply(pair):
    matrices, arriving = pair
    mats = matrices.astype(jnp.float32)
    inflow = arriving.astype(jnp.float32)
    real_part = jnp.einsum("fij,fjp->fip", mats[:, 0], inflow[0]) - jnp.einsum("fij,fjp->fip", mats[:, 1], inflow[1])
    imag_part = jnp.einsum("fij,fjp->fip", mats[:, 0], inflow[1]) + jnp.einsum("fij,fjp->fip", mats[:, 1], inflow[0])
    return jnp.stack([real_part, imag_part])


def reference(interface_op, mortar, source, trace_len, corner_rows, corner_owner, coarse_inv):
    rows_count, cols_count = interface_op.shape[0], interface_op.shape[1]
    subs = rows_count * cols_count
    order = interface_op.shape[-1]
    face = order // 4
    ports = source.shape[-1]
    ops_flat = interface_op.reshape(subs, 2, order, order)
    mortar_flat = mortar.reshape(subs, 4, 2, face, face)
    rows_flat = corner_rows.reshape(subs, -1).astype(jnp.int32)
    owner_flat = corner_owner.reshape(-1).astype(jnp.int32)
    keep = (jnp.arange(face, dtype=jnp.int32)[None, None, None, :] < trace_len[:, :, :, None]).astype(jnp.float32)
    field = source
    history = []
    for iteration in range(ITERS):
        field_low = field.astype(jnp.bfloat16).reshape(subs, 2, order, ports)
        product = lax.map(lambda pair: complex_dot(pair[0], pair[1]), (ops_flat, field_low))
        faces = product.reshape(rows_count, cols_count, 2, 4, face, ports) * keep[:, :, None, :, :, None]
        faces_out = faces.astype(jnp.bfloat16)
        in_zero = jnp.concatenate([jnp.zeros_like(faces_out[:1, :, :, 1]), faces_out[:-1, :, :, 1]], 0)
        in_one = jnp.concatenate([faces_out[1:, :, :, 0], jnp.zeros_like(faces_out[:1, :, :, 0])], 0)
        in_two = jnp.concatenate([jnp.zeros_like(faces_out[:, :1, :, 3]), faces_out[:, :-1, :, 3]], 1)
        in_three = jnp.concatenate([faces_out[:, 1:, :, 2], jnp.zeros_like(faces_out[:, :1, :, 2])], 1)
        incoming = jnp.stack([in_zero, in_one, in_two, in_three], 3).reshape(subs, 2, 4, face, ports)
        coupled = lax.map(mortar_apply, (mortar_flat, incoming)).reshape(subs, 2, order, ports)
        corner_vals = jax.vmap(lambda whole, picks: whole[:, picks])(product, rows_flat)
        spread = jnp.transpose(corner_vals, (1, 0, 2, 3)).reshape(2, -1, ports)
        coarse_vec = jnp.zeros((2, coarse_inv.shape[-1], ports), jnp.float32).at[:, owner_flat].add(spread)
        coarse_sol = complex_dot(coarse_inv, coarse_vec, lax.Precision.HIGHEST)
        back = jnp.transpose(coarse_sol[:, owner_flat].reshape(2, subs, -1, ports), (1, 0, 2, 3))
        correction = jax.vmap(lambda picks, values: jnp.zeros((2, order, ports), jnp.float32).at[:, picks].add(values))(rows_flat, back)
        fresh = source.reshape(subs, 2, order, ports) + 0.5 * coupled - correction
        change = fresh - field.reshape(subs, 2, order, ports)
        history.append(jnp.sum(change * change, axis=(0, 1, 2)))
        field = fresh.reshape(source.shape)
    return field, jnp.stack(history)
```

```python
import jax
import jax.numpy as jnp
from jax import lax
from jax.sharding import PartitionSpec as P

ITERS = 3
ALL = ("region", "nbr")


def shifted(value, axis, by):
    size = lax.axis_size(axis)
    pairs = [(i, i + by) for i in range(size) if 0 <= i + by < size]
    return lax.ppermute(value, axis, pairs)


def complex_dot(left, right, accuracy=None):
    def dot(a, b):
        return jnp.dot(a, b, preferred_element_type=jnp.float32, precision=accuracy)

    real_part = dot(left[0], right[0]) - dot(left[1], right[1])
    imag_part = dot(left[0], right[1]) + dot(left[1], right[0])
    return jnp.stack([real_part, imag_part])


def swap(rows):
    return lax.all_to_all(rows, ALL, 0, 0, tiled=True)


def shards(interface_op, mortar, source, trace_len, corner_rows, corner_owner, coarse_inv):
    operator = interface_op[0, 0]
    mortars = mortar[0, 0]
    excitation = source[0, 0]
    lengths = trace_len[0, 0]
    picks = corner_rows[0, 0]
    owners = corner_owner[0, 0]
    order = operator.shape[-1]
    face = order // 4
    ports = excitation.shape[-1]
    corners = owners.shape[0]
    coarse_count = coarse_inv.shape[-1]
    devices = lax.axis_size("region") * lax.axis_size("nbr")
    held = ports // devices
    highest = lax.Precision.HIGHEST
    selector = (picks[:, None] == jnp.arange(order, dtype=jnp.int32)[None, :]).astype(jnp.float32)
    keep = (jnp.arange(face, dtype=jnp.int32)[None, :] < lengths[:, None]).astype(jnp.float32)
    field = excitation
    table = None
    history = []
    for iteration in range(ITERS):
        field_low = field.astype(jnp.bfloat16)
        product = complex_dot(operator, field_low)
        faces_out = (product.reshape(2, 4, face, ports) * keep[None, :, :, None]).astype(
            jnp.bfloat16
        )
        in_two = shifted(faces_out[:, 3], "nbr", 1)
        in_three = shifted(faces_out[:, 2], "nbr", -1)
        in_zero = shifted(faces_out[:, 1], "region", 1)
        in_one = shifted(faces_out[:, 0], "region", -1)
        corner_vals = jnp.einsum("kn,cnp->kcp", selector, product, precision=highest)
        rows = corner_vals.reshape(corners * 2, devices, held).transpose(1, 0, 2)
        rows = rows.reshape(devices, corners * 2 * held)
        if table is None:
            extra = jnp.broadcast_to(owners.astype(jnp.float32)[None, :], (devices, corners))
            got = swap(jnp.concatenate([rows, extra], 1))
            all_owners = got[:, corners * 2 * held :].reshape(-1).astype(jnp.int32)
            table = (
                all_owners[:, None] == jnp.arange(coarse_count, dtype=jnp.int32)[None, :]
            ).astype(jnp.float32)
            got = got[:, : corners * 2 * held]
        else:
            got = swap(rows)
        values = got.reshape(devices * corners, 2 * held)
        added = jnp.dot(values.T, table, precision=highest).reshape(2, held, coarse_count)
        inv_t = jnp.swapaxes(coarse_inv, 1, 2)
        sol_r = jnp.dot(added[0], inv_t[0], precision=highest) - jnp.dot(
            added[1], inv_t[1], precision=highest
        )
        sol_i = jnp.dot(added[0], inv_t[1], precision=highest) + jnp.dot(
            added[1], inv_t[0], precision=highest
        )
        sol = jnp.concatenate([sol_r, sol_i], 0)
        picked = lax.dot_general(
            table, sol, (((1,), (1,)), ((), ())), precision=highest
        ).reshape(devices, corners * 2 * held)
        back = swap(picked).reshape(devices, corners, 2, held)
        back = back.transpose(2, 1, 0, 3).reshape(2, corners, ports)
        incoming = jnp.stack([in_zero, in_one, in_two, in_three], 1)

        def apply(m, x):
            return jnp.einsum("fij,fjp->fip", m, x, preferred_element_type=jnp.float32)

        real_part = apply(mortars[:, 0], incoming[0]) - apply(mortars[:, 1], incoming[1])
        imag_part = apply(mortars[:, 0], incoming[1]) + apply(mortars[:, 1], incoming[0])
        coupled = jnp.stack([real_part, imag_part]).reshape(2, order, ports)
        correction = jnp.einsum("kn,ckp->cnp", selector, back, precision=highest)
        fresh = excitation + 0.5 * coupled - correction
        change = fresh - field
        history.append(jnp.sum(change * change, axis=(0, 1)))
        field = fresh
    increments = jnp.stack(history).reshape(1, -1)
    spread = jnp.broadcast_to(increments, (devices, increments.shape[1]))
    increments = jnp.sum(swap(spread), 0).reshape(ITERS, ports)
    return (field[None, None], increments)


def solution(mesh):
    placed = (
        P("region", "nbr", None, None, None),
        P("region", "nbr", None, None, None, None),
        P("region", "nbr", None, None, None),
        P("region", "nbr", None),
        P("region", "nbr", None),
        P("region", "nbr", None),
        P(),
    )
    return jax.shard_map(
        shards,
        mesh=mesh,
        in_specs=placed,
        out_specs=(P("region", "nbr", None, None, None), P()),
        check_vma=False,
    )
```

```python
import functools

import jax
import jax.numpy as jnp
from jax import lax
from jax.experimental import pallas as pl
from jax.experimental.pallas import tpu as pltpu
from jax.sharding import PartitionSpec as P


ITERS = 3
ALL = ("region", "nbr")
FACES = 4
C = 8
F32 = jnp.float32
BF16 = jnp.bfloat16

H0, B1, B2, G0R, G1R, OWN = 0, 16, 80, 144, 272, 784
ROWS_OUT = 1024
BACK = 384


def nn(a, b):
    return lax.dot_general(a, b, (((1,), (0,)), ((), ())), preferred_element_type=F32)


def nt(a, b):
    return lax.dot_general(a, b, (((1,), (1,)), ((), ())), preferred_element_type=F32)


def tn(a, b):
    return lax.dot_general(a, b, (((0,), (0,)), ((), ())), preferred_element_type=F32)


def skinny(rows, real, imag, dot):
    half = rows.shape[0] // 2
    p, q = dot(rows, real), dot(rows, imag)
    return p[:half] - q[half:], p[half:] + q[:half]


def wide(real, imag, both, n):
    a, b = nn(real, both), nn(imag, both)
    return a[:, :n] - b[:, n:], a[:, n:] + b[:, :n]


def both_parts(top, low):
    return jnp.concatenate([top, low], 0)


def op_copy(op_hbm, op_v, sem, f, face):
    rows = pl.ds(f * face, face)
    return pltpu.make_async_copy(op_hbm.at[:, rows, :], op_v.at[:, rows, :], sem.at[f])


def lane_keep(x, length):
    lane = lax.broadcasted_iota(jnp.int32, x.shape, 1)
    return jnp.where(lane < length, x, 0.0)


def row_keep(x, length):
    row = lax.broadcasted_iota(jnp.int32, x.shape, 0)
    return jnp.where(row < length, x, 0.0).astype(BF16)


def first_kernel(lens, picks, s_ref, op_hbm, mor_hbm, m0, m1, m2, m3, h0_ref, g0_ref,
                 op_v, mor_v, x_v, sem, msem):
    face, n = op_v.shape[1] // FACES, s_ref.shape[2]
    order = op_v.shape[1]
    for f in range(FACES):
        op_copy(op_hbm, op_v, sem, f, face).start()
    mcopy = pltpu.make_async_copy(mor_hbm, mor_v, msem)
    mcopy.start()
    x_v[:, :n] = s_ref[0].astype(BF16)
    x_v[:, n:] = s_ref[1].astype(BF16)
    row = lax.broadcasted_iota(jnp.int32, (2 * C, order), 0)
    lane = lax.broadcasted_iota(jnp.int32, (2 * C, order), 1)
    spot = jnp.full((2 * C, order), -1, jnp.int32)
    for k in range(C):
        spot = jnp.where(row == k, picks[k], spot)
    sel = jnp.where(lane == spot, 1.0, 0.0).astype(BF16)
    outs = (m0, m1, m2, m3)
    rr = jnp.zeros((2 * C, order), F32)
    ri = jnp.zeros((2 * C, order), F32)
    q = []
    for f in range(FACES):
        op_copy(op_hbm, op_v, sem, f, face).wait()
        rows = slice(f * face, (f + 1) * face)
        re, im = wide(op_v[0, rows], op_v[1, rows], x_v[...], n)
        outs[f][0, :face] = row_keep(re, lens[f])
        outs[f][1, :face] = row_keep(im, lens[f])
        q.append([lane_keep(nt(sel, op_v[c, rows])[:C], lens[f]) for c in (0, 1)])
        rr = rr + nn(sel[:, rows], op_v[0, rows])
        ri = ri + nn(sel[:, rows], op_v[1, rows])
    rop = both_parts(rr[:C], ri[:C]).astype(BF16)
    p = nn(rop, x_v[...])
    h0_ref[:C] = p[:C, :n] - p[C:, n:]
    h0_ref[C:] = p[:C, n:] + p[C:, :n]
    g0_ref[...] = nt(sel, rop)
    mcopy.wait()
    for f in range(FACES):
        rows = slice(f * face, (f + 1) * face)
        b_re, b_im = skinny(rop[:, rows], mor_v[f, 0], mor_v[f, 1], nn)
        outs[f][0, face:] = both_parts(0.5 * b_re, q[f][0]).astype(BF16)
        outs[f][1, face:] = both_parts(0.5 * b_im, q[f][1]).astype(BF16)


def fresh_faces(ins, mor_v, s_ref, u_ref, x_v, face, n):
    for f in range(FACES):
        rows = slice(f * face, (f + 1) * face)
        xr, xi = ins[f][0, :face], ins[f][1, :face]
        re = s_ref[0, rows] + 0.5 * (nn(mor_v[f, 0], xr) - nn(mor_v[f, 1], xi))
        im = s_ref[1, rows] + 0.5 * (nn(mor_v[f, 0], xi) + nn(mor_v[f, 1], xr))
        u_ref[0, rows] = re
        u_ref[1, rows] = im
        if x_v is not None:
            x_v[rows, :n] = re.astype(BF16)
            x_v[rows, n:] = im.astype(BF16)


def second_kernel(lens, owners, i0, i1, i2, i3, o0, o1, o2, o3, s_ref, h0_ref, g0_ref,
                  op_hbm, mor_hbm, m0, m1, m2, m3, u_ref, t1_ref, pay_ref,
                  op_v, mor_v, x_v, p_v, sem, msem):
    face, n = op_v.shape[1] // FACES, s_ref.shape[2]
    mcopy = pltpu.make_async_copy(mor_hbm, mor_v, msem)
    mcopy.start()
    for f in range(FACES):
        op_copy(op_hbm, op_v, sem, f, face).start()
    ins, owns, outs = (i0, i1, i2, i3), (o0, o1, o2, o3), (m0, m1, m2, m3)
    mcopy.wait()
    fresh_faces(ins, mor_v, s_ref, u_ref, x_v, face, n)
    p_v[H0:B1] = h0_ref[...]
    t1, nb = [], []
    for f in range(FACES):
        tail = [ins[f][c, face:].astype(F32) for c in (0, 1)]
        mine = [owns[f][c, face:].astype(F32) for c in (0, 1)]
        t_re, t_im = skinny(
            both_parts(tail[0][C:], tail[1][C:]).astype(BF16), mor_v[f, 0], mor_v[f, 1], nt
        )
        t1.append(both_parts(0.5 * t_re, 0.5 * t_im).astype(BF16))
        t1_ref[f] = t1[f]
        b = both_parts(tail[0][:C], tail[1][:C]).astype(BF16)
        nb.append(b)
        re, im = skinny(b, owns[f][0, :face], owns[f][1, :face], nn)
        p_v[B1 + 16 * f : B1 + 16 * f + C] = re
        p_v[B1 + 16 * f + C : B1 + 16 * f + 16] = im
        g = nt(both_parts(mine[0][C:], mine[1][C:]).astype(BF16), b)
        g_re = g[:C, :C] - g[C:, C:]
        g_im = g[:C, C:] + g[C:, :C]
        for k in range(C):
            at = G1R + 128 * f + 16 * k
            p_v[at : at + C] = jnp.broadcast_to(g_re[:, k : k + 1], (C, n))
            p_v[at + C : at + 16] = jnp.broadcast_to(g_im[:, k : k + 1], (C, n))
    g0 = g0_ref[...]
    for k in range(C):
        at = G0R + 16 * k
        p_v[at : at + C] = jnp.broadcast_to(g0[:C, k : k + 1], (C, n))
        p_v[at + C : at + 16] = jnp.broadcast_to(g0[:C, C + k : C + k + 1], (C, n))
    row = lax.broadcasted_iota(jnp.int32, (C, n), 0)
    own = jnp.zeros((C, n), F32)
    for k in range(C):
        own = jnp.where(row == k, owners[k].astype(F32), own)
    p_v[OWN : OWN + C] = own
    p_v[OWN + C :] = jnp.zeros((ROWS_OUT - OWN - C, n), F32)
    extra = []
    for f in range(FACES):
        op_copy(op_hbm, op_v, sem, f, face).wait()
        rows = slice(f * face, (f + 1) * face)
        re, im = wide(op_v[0, rows], op_v[1, rows], x_v[...], n)
        low_re, low_im = row_keep(re, lens[f]), row_keep(im, lens[f])
        outs[f][0, :face] = low_re
        outs[f][1, :face] = low_im
        re, im = skinny(nb[f], low_re, low_im, nn)
        p_v[B2 + 16 * f : B2 + 16 * f + C] = re
        p_v[B2 + 16 * f + C : B2 + 16 * f + 16] = im
    for g in range(FACES):
        out_rows = slice(g * face, (g + 1) * face)
        parts = []
        for f in range(FACES):
            cols = slice(f * face, (f + 1) * face)
            parts.append(skinny(t1[f], op_v[0, out_rows, cols], op_v[1, out_rows, cols], nt))
        for c in (0, 1):
            stacked = jnp.concatenate([part[c] for part in parts], 0)
            outs[g][c, face:] = lane_keep(stacked, lens[g]).astype(BF16)
    for j in range(ROWS_OUT // 128):
        pay_ref[pl.ds(j, n, stride=ROWS_OUT // 128), :] = p_v[128 * j : 128 * (j + 1)].T


def third_kernel(lens, i0, i1, i2, i3, s_ref, op_hbm, mor_hbm, m0, m1, m2, m3, u_ref, t2_ref,
                 op_v, mor_v, x_v, sem, msem):
    face, n = op_v.shape[1] // FACES, s_ref.shape[2]
    mcopy = pltpu.make_async_copy(mor_hbm, mor_v, msem)
    mcopy.start()
    for f in range(FACES):
        op_copy(op_hbm, op_v, sem, f, face).start()
    ins, outs = (i0, i1, i2, i3), (m0, m1, m2, m3)
    mcopy.wait()
    fresh_faces(ins, mor_v, s_ref, u_ref, x_v, face, n)
    for f in range(FACES):
        op_copy(op_hbm, op_v, sem, f, face).wait()
        rows = slice(f * face, (f + 1) * face)
        re, im = wide(op_v[0, rows], op_v[1, rows], x_v[...], n)
        outs[f][0] = row_keep(re, lens[f])
        outs[f][1] = row_keep(im, lens[f])
    for f in range(FACES):
        tail = both_parts(ins[f][0, face:], ins[f][1, face:])
        t_re, t_im = skinny(tail, mor_v[f, 0], mor_v[f, 1], nt)
        t2_ref[f] = both_parts(0.5 * t_re, 0.5 * t_im).astype(BF16)


def pick_lanes(values, index):
    rows, n = index.shape
    count = values.shape[1]
    step = min(128, n)
    out = []
    for a in range(0, n, step):
        idx = index[:, a : a + step]
        got = jnp.zeros((rows, step), F32)
        for b in range(0, count, step):
            table = jnp.broadcast_to(values[:, b : b + step], (rows, step))
            inside = jnp.logical_and(idx >= b, idx < b + step)
            local = jnp.where(inside, idx - b, 0)
            got = jnp.where(inside, jnp.take_along_axis(table, local, axis=1), got)
        out.append(got)
    return jnp.concatenate(out, 1)


def split_low(x):
    high = x.astype(BF16)
    return high, (x - high.astype(F32)).astype(BF16)


def coarse_kernel(nbr, got_ref, inv_ref, back_ref, v_v, hot_v, f_v, o_v):
    n = v_v.shape[1]
    count = inv_ref.shape[1]
    per = ROWS_OUT // 128
    f_v[...] = got_ref[...].astype(F32)
    for j in range(OWN // 128 + 1):
        v_v[128 * j : 128 * (j + 1)] = f_v[pl.ds(j, n, stride=per), :].T
    owner = v_v[OWN : OWN + C].astype(jnp.int32)
    coarse = lax.broadcasted_iota(jnp.int32, (count, n), 0)
    for l in range(C):
        hot_v[l] = jnp.where(coarse == owner[l : l + 1], 1.0, 0.0).astype(BF16)
    toward = (-nbr, nbr, -1, 1)

    def moved(x, by):
        by = by % n
        return pltpu.roll(x, by, 1) if by else x

    sub = lax.broadcasted_iota(jnp.int32, (C, n), 0)

    def scatter(arrays):
        total = None
        for l in range(C):
            rows = []
            for a in arrays:
                high, low = split_low(jnp.where(sub == l, a, 0.0))
                rows += [high.astype(F32), low.astype(F32)]
            part = nt(jnp.concatenate(rows, 0).astype(BF16), hot_v[l])
            total = part if total is None else total + part
        return [
            jnp.sum(total[2 * C * a : 2 * C * (a + 1)], axis=0, keepdims=True)
            for a in range(len(arrays))
        ]

    sub8 = lax.broadcasted_iota(jnp.int32, (8, count), 0)

    def solve(g):
        lhs = jnp.where(sub8 == 0, g[0], jnp.where(sub8 == 1, g[1], 0.0))

        def dot(b):
            return lax.dot_general(
                lhs, b, (((1,), (1,)), ((), ())), preferred_element_type=F32,
                precision=lax.Precision.HIGHEST,
            )

        a, b = dot(inv_ref[0]), dot(inv_ref[1])
        return a[0:1] - b[1:2], a[1:2] + b[0:1]

    def block(at, q):
        out_re = jnp.zeros((C, n), F32)
        out_im = jnp.zeros((C, n), F32)
        for k in range(C):
            re = v_v[at + 16 * k : at + 16 * k + C]
            im = v_v[at + 16 * k + C : at + 16 * k + 16]
            s_re = jnp.sum(re * q[0] - im * q[1], axis=0, keepdims=True)
            s_im = jnp.sum(re * q[1] + im * q[0], axis=0, keepdims=True)
            out_re = jnp.where(sub == k, s_re, out_re)
            out_im = jnp.where(sub == k, s_im, out_im)
        return out_re, out_im

    def gather(c):
        return pick_lanes(c[0], owner), pick_lanes(c[1], owner)

    h0 = (v_v[H0 : H0 + C], v_v[H0 + C : H0 + 16])
    gamma = [h0]
    for base in (B1, B2):
        parts = []
        for c in (0, 1):
            x = h0[c]
            for f in range(FACES):
                at = base + 16 * f + C * c
                x = x + moved(v_v[at : at + C], toward[f])
            parts.append(x)
        gamma.append(tuple(parts))
    sums = scatter([part for pair in gamma for part in pair])
    c0 = solve(sums[0:2])
    q0 = gather(c0)
    y = block(G0R, q0)
    less = scatter(list(y))
    c1 = solve([sums[2] - less[0], sums[3] - less[1]])
    q1 = gather(c1)
    y = block(G0R, q1)
    y_re, y_im = y
    for f in range(FACES):
        z = block(G1R + 128 * f, q0)
        y_re = y_re + moved(z[0], toward[f])
        y_im = y_im + moved(z[1], toward[f])
    less = scatter([y_re, y_im])
    c2 = solve([sums[4] - less[0], sums[5] - less[1]])
    q2 = gather(c2)
    for slot, (which, by) in enumerate(back_slots(nbr)):
        q = (q0, q1, q2)[which]
        for c in (0, 1):
            at = 2 * C * slot + C * c
            o_v[at : at + C] = moved(q[c], -by)
    used = 2 * C * len(back_slots(nbr))
    o_v[used:] = jnp.zeros((o_v.shape[0] - used, n), F32)
    per = o_v.shape[0] // 128
    for j in range(per):
        back_ref[pl.ds(j, n, stride=per), :] = o_v[128 * j : 128 * (j + 1)].T


def back_slots(nbr):
    toward = (-nbr, nbr, -1, 1)
    slots = [(0, 0), (1, 0), (2, 0)]
    slots += [(0, t) for t in toward] + [(1, t) for t in toward]
    for a in toward:
        for b in toward:
            if (0, a + b) not in slots:
                slots.append((0, a + b))
    return slots


def last_kernel(nbr, picks, i0, i1, i2, i3, s_ref, u1_ref, u2_ref, t1_ref, t2_ref, got_ref, mor_v,
                field_ref, inc_ref, f_v, q_v, w1, w2, w3):
    face, n = s_ref.shape[1] // FACES, s_ref.shape[2]
    ins = (i0, i1, i2, i3)
    per = q_v.shape[0] // 128
    f_v[...] = got_ref[...].astype(F32)
    for j in range(per):
        q_v[128 * j : 128 * (j + 1)] = f_v[pl.ds(j, n, stride=per), :].T
    slots = back_slots(nbr)
    toward = (-nbr, nbr, -1, 1)

    def q(which, by):
        at = 2 * C * slots.index((which, by))
        return q_v[at : at + C], q_v[at + C : at + 2 * C]

    def rhs(pairs):
        re = jnp.concatenate([p[0] for p in pairs], 0)
        im = jnp.concatenate([p[1] for p in pairs], 0)
        return jnp.concatenate(
            [jnp.concatenate([re, im], 1), jnp.concatenate([-im, re], 1)], 0
        ).astype(BF16)

    zero = jnp.zeros((face, n), F32)
    for f in range(FACES):
        rows = slice(f * face, (f + 1) * face)
        a = tn(t1_ref[f], rhs([q(0, toward[f])]))
        w2[0, rows] = a[:, :n]
        w2[1, rows] = a[:, n:]
        b = tn(t2_ref[f], rhs([q(0, toward[f] + t) for t in toward]))
        b = b + tn(t1_ref[f], rhs([q(1, toward[f])]))
        w3[0, rows] = b[:, :n]
        w3[1, rows] = b[:, n:]
        w1[0, rows] = zero
        w1[1, rows] = zero
    for which, w in enumerate((w1, w2, w3)):
        parts = q(which, 0)
        for c in (0, 1):
            for k in range(C):
                at = pl.ds(picks[k], 1)
                w[c, at, :] = w[c, at, :] + parts[c][k : k + 1]
    sums = [jnp.zeros((8, n), F32) for _ in range(ITERS)]

    def add(total, x):
        return total + jnp.sum((x * x).reshape(face // 8, 8, n), axis=0)

    for f in range(FACES):
        rows = slice(f * face, (f + 1) * face)
        xr, xi = ins[f][0], ins[f][1]
        m_re, m_im = mor_v[f, 0], mor_v[f, 1]
        for c in (0, 1):
            s = s_ref[c, rows]
            if c == 0:
                u3 = s + 0.5 * (nn(m_re, xr) - nn(m_im, xi))
            else:
                u3 = s + 0.5 * (nn(m_re, xi) + nn(m_im, xr))
            f1 = u1_ref[c, rows] - w1[c, rows]
            f2 = u2_ref[c, rows] - w2[c, rows]
            f3 = u3 - w3[c, rows]
            field_ref[c, rows] = f3
            sums[0] = add(sums[0], f1 - s)
            sums[1] = add(sums[1], f2 - f1)
            sums[2] = add(sums[2], f3 - f2)
    rows = [jnp.sum(x, axis=0, keepdims=True) for x in sums]
    inc_ref[...] = jnp.concatenate(rows + [jnp.zeros((8 - ITERS, n), F32)], 0)


def shifted(value, axis, by):
    size = lax.axis_size(axis)
    pairs = [(i, i + by) for i in range(size) if 0 <= i + by < size]
    return lax.ppermute(value, axis, pairs)


def exchange(msgs):
    two = shifted(msgs[3], "nbr", 1)
    three = shifted(msgs[2], "nbr", -1)
    zero = shifted(msgs[1], "region", 1)
    one = shifted(msgs[0], "region", -1)
    return [zero, one, two, three]


def swap(blocks):
    return lax.all_to_all(blocks, ALL, 0, 0, tiled=True)


VMEM = pl.BlockSpec(memory_space=pltpu.VMEM)
SMEM = pl.BlockSpec(memory_space=pltpu.SMEM)
ANY = pl.BlockSpec(memory_space=pl.ANY)


def call(kernel, args, specs, outs, scratch, name, flops, nbytes):
    return pl.pallas_call(
        kernel,
        out_shape=[jax.ShapeDtypeStruct(*o) for o in outs],
        in_specs=specs,
        out_specs=[VMEM] * len(outs),
        scratch_shapes=scratch,
        name=name,
        cost_estimate=pl.CostEstimate(flops=flops, bytes_accessed=nbytes, transcendentals=0),
    )(*args)


def shards(interface_op, mortar, source, trace_len, corner_rows, corner_owner, coarse_inv):
    op, mor, s = interface_op[0, 0], mortar[0, 0], source[0, 0]
    lens, picks, owners = trace_len[0, 0], corner_rows[0, 0], corner_owner[0, 0]
    order, n = s.shape[1], s.shape[2]
    face = order // FACES
    nbr = lax.axis_size("nbr")
    devices = lax.axis_size("region") * nbr
    assert n == devices and owners.shape[0] == C
    op_scr = [
        pltpu.VMEM((2, order, order), BF16),
        pltpu.VMEM((FACES, 2, face, face), BF16),
        pltpu.VMEM((order, 2 * n), BF16),
    ]
    sems = [pltpu.SemaphoreType.DMA((FACES,)), pltpu.SemaphoreType.DMA]
    work = 8 * order * order * n
    load = 4 * order * order + 8 * face * face * FACES + 8 * order * n

    def msg(extra):
        return [((2, face + extra, n), BF16)] * FACES

    field = ((2, order, n), F32)
    *sent1, h0, g0 = call(
        first_kernel, (lens, picks, s, op, mor), [SMEM, SMEM, VMEM, ANY, ANY],
        msg(2 * C) + [((2 * C, n), F32), ((2 * C, 2 * C), F32)],
        op_scr + sems, "first", work, load,
    )
    in1 = exchange(sent1)
    *sent2, u1, t1, pay = call(
        second_kernel, (lens, owners, *in1, *sent1, s, h0, g0, op, mor),
        [SMEM, SMEM] + [VMEM] * 11 + [ANY, ANY],
        msg(FACES * C) + [field, ((FACES, 2 * C, face), BF16), ((devices * ROWS_OUT // 128, 128), F32)],
        op_scr + [pltpu.VMEM((ROWS_OUT, n), F32)] + sems, "second", work + work // 4, 2 * load,
    )
    in2 = exchange(sent2)
    got = swap(pay.astype(BF16).reshape(devices, ROWS_OUT // 128, 128))
    *sent3, u2, t2 = call(
        third_kernel, (lens, *in2, s, op, mor), [SMEM] + [VMEM] * 5 + [ANY, ANY],
        msg(0) + [field, ((FACES, 2 * FACES * C, face), BF16)],
        op_scr + sems, "third", work + work // 4, 2 * load,
    )
    in3 = exchange(sent3)
    (back,) = call(
        functools.partial(coarse_kernel, nbr), (got.reshape(-1, 128), coarse_inv), [VMEM] * 2,
        [((devices * BACK // 128, 128), F32)],
        [
            pltpu.VMEM((ROWS_OUT, devices), F32),
            pltpu.VMEM((C, coarse_inv.shape[1], devices), BF16),
            pltpu.VMEM((devices * ROWS_OUT // 128, 128), F32),
            pltpu.VMEM((BACK, devices), F32),
        ],
        "coarse", work // 2, 1 << 21,
    )
    got2 = swap(back.astype(BF16).reshape(devices, BACK // 128, 128))
    final, inc = call(
        functools.partial(last_kernel, nbr),
        (picks, *in3, s, u1, u2, t1, t2, got2.reshape(-1, 128), mor),
        [SMEM] + [VMEM] * 11,
        [field, ((8, n), F32)],
        [
            pltpu.VMEM((devices * BACK // 128, 128), F32),
            pltpu.VMEM((BACK, n), F32),
        ] + [pltpu.VMEM((2, order, n), F32)] * 3,
        "last", work // 4, 10 * order * n * 4,
    )
    spread = jnp.broadcast_to(
        inc.reshape(1, -1, min(128, n)).astype(BF16)[:, :8], (devices, 8, min(128, n))
    )
    increments = jnp.sum(swap(spread).astype(F32), 0).reshape(-1, n)[:ITERS]
    return (final[None, None], increments)


def solution(mesh):
    placed = (
        P("region", "nbr", None, None, None),
        P("region", "nbr", None, None, None, None),
        P("region", "nbr", None, None, None),
        P("region", "nbr", None),
        P("region", "nbr", None),
        P("region", "nbr", None),
        P(),
    )
    return jax.shard_map(
        shards,
        mesh=mesh,
        in_specs=placed,
        out_specs=(P("region", "nbr", None, None, None), P()),
        check_vma=False,
    )
```
